768 devices in a mesh: rows: 12 (over z), cols: 64 (over x, y, core).
Axes of the slice: x: 4, y: 8, z: 12, core: 2. Of those that a mesh axis runs over, the one named last changes fastest.
Arguments:
- tile_values: bfloat16 [12, 64, 4, 128, 128], P('rows', 'cols'), may hold values from 0.0009994507 to 0.019897461
- tile_rows: int32 [12, 64, 4], P('rows', 'cols'), may hold values from 0 to 7, as said below
- tile_cols: int32 [12, 64, 4], P('rows', 'cols'), may hold values from 0 to 3, as said below
- live_counts: int32 [12, 64], P('rows', 'cols'), may hold values from 1 to 4, as said below
- test_block: float32 [32768, 512], P('cols'), may hold values from -6 to 6
Outputs:
- y_sample: float32 [12288, 512], P(('rows', 'cols'))
- z_power: float32 [32768, 512], P('cols')
- panel_gram: float32 [12, 512, 512], P('rows')
The draws below stay inside these ranges and needn't reach their ends.
Inputs may be any that keep to these rules, and one draw needn't show every extreme that they name: Within one device the pairs (tile_rows, tile_cols) of its slots are distinct. `tile_cols`: column block of a slot within the device's columns. `live_counts`: some device uses all 4 slots.
All inputs are finite; a program needn't handle non-finite values.
Results may differ from the reference program's by a relative error of at most 0.0003.
Values sent between devices are 32-bit elements; how exact they have to be, the bound alone decides.
No kernel may reach another device: no remote copies, remote signals or barrier semaphores. Data moves between devices by JAX's collectives and lax.ppermute only.
A program may use at most 32 MiB of HBM per device.

```python
import math
import jax
import jax.numpy as jnp
from jax import lax

TEST_K = 512
RB_DEV = 8
CB_DEV = 4
NB_DEV = 4
CONTEXTS = 32768
N_ROWS = 12
N_COLS = 64


def slot_positions(key):
    keys = jax.random.split(jax.random.fold_in(key, 11), N_ROWS * N_COLS)
    orders = jax.vmap(lambda single: jax.random.permutation(single, RB_DEV * CB_DEV))(keys)
    return orders[:, :NB_DEV].reshape(N_ROWS, N_COLS, NB_DEV).astype(jnp.int32)


def draw_tile_rows(key, part):
    return (slot_positions(key) // CB_DEV).astype(jnp.int32)


def draw_tile_cols(key, part):
    return (slot_positions(key) % CB_DEV).astype(jnp.int32)


def draw_live_counts(key, part):
    lowest = max(NB_DEV // 4, 1)
    total = N_ROWS * N_COLS
    counts = jax.random.randint(jax.random.fold_in(key, 23), (total,), lowest, NB_DEV + 1)
    picks = jax.random.randint(jax.random.fold_in(key, 29), (2,), 0, total)
    places = jnp.arange(total, dtype=jnp.int32)
    counts = jnp.where(places == picks[0], NB_DEV, counts)
    counts = jnp.where((places == picks[1]) & (picks[1] != picks[0]), lowest, counts)
    return counts.reshape(N_ROWS, N_COLS).astype(jnp.int32)


def levels(key, extent, cuts, smallest, largest):
    level, own = 1.0, jax.random.fold_in(key, 6)
    for position, parts in cuts:
        heights = jnp.exp(jax.random.uniform(jax.random.fold_in(own, position), (parts,), jnp.float32, smallest / len(cuts), largest / len(cuts)))
        level = level * jnp.repeat(heights, extent[position] // parts).reshape([-1 if axis == position else 1 for axis in range(len(extent))])
    return level


def gaussian(rng, dims, width, limit, shards=(), kind=jnp.bfloat16):
    loudness = levels(rng, dims, shards, -0.22, 0.18) if shards else 1.0
    result = jax.random.normal(rng, dims, jnp.float32) * width * loudness
    return jnp.minimum(jnp.maximum(result, -limit), limit).astype(kind)


def setup_inputs(seed: int = 0) -> dict:
    splits = jax.random.split(jax.random.key(seed), 6)
    tile_values = jnp.clip(jnp.exp(math.log(0.019897461) - 2.9911416 * jax.random.uniform(splits[0], (N_ROWS, N_COLS, NB_DEV, 128, 128), jnp.float32) ** levels(splits[0], (N_ROWS, N_COLS, NB_DEV, 128, 128), ((0, 12), (1, 64)), -0.2, 0.2)), 0.0009994507, 0.019897461).astype(jnp.bfloat16)
    tile_rows = draw_tile_rows(jax.random.fold_in(splits[5], 71), 0)
    tile_cols = draw_tile_cols(jax.random.fold_in(splits[5], 71), 0)
    live_counts = draw_live_counts(jax.random.fold_in(splits[5], 71), 0)
    test_block = gaussian(splits[4], (CONTEXTS, TEST_K), 1.0, 6.0, ((0, 64),), jnp.float32)
    return {"tile_values": tile_values, "tile_rows": tile_rows, "tile_cols": tile_cols, "live_counts": live_counts, "test_block": test_block}


def reference(tile_values, tile_rows, tile_cols, live_counts, test_block):
    test_cols = test_block.shape[1]
    omega_tiles = test_block.reshape(N_COLS * CB_DEV, 128, test_cols)
    slot_index = jnp.arange(NB_DEV, dtype=jnp.int32)
    col_base = (CB_DEV * jnp.arange(N_COLS, dtype=jnp.int32))[:, None]
    high = lax.Precision.HIGHEST

    def row_panel(z_total, inputs):
        tile_data, rows_local, cols_local, counts = inputs
        keep_mask = (slot_index[None, :] < counts[:, None]).astype(jnp.float32)
        global_cols = (cols_local + col_base).astype(jnp.int32)
        tiles_f = tile_data.astype(jnp.float32) * keep_mask[:, :, None, None]
        picked = omega_tiles[global_cols]
        products = jnp.einsum("csab,csbk->csak", tiles_f, picked, precision=high)
        onehot = (rows_local[:, :, None] == jnp.arange(RB_DEV, dtype=jnp.int32)[None, None, :]).astype(jnp.float32)
        y_blocks = jnp.einsum("csr,csak->rak", onehot, products, precision=high)
        y_tiles = y_blocks[rows_local]
        z_terms = jnp.einsum("csab,csak->csbk", tiles_f, y_tiles, precision=high)
        z_total = z_total.at[global_cols].add(z_terms)
        y_panel = y_blocks.reshape(RB_DEV * 128, test_cols)
        gram = jnp.dot(y_panel.T, y_panel, precision=high, preferred_element_type=jnp.float32) / (RB_DEV * 128)
        return z_total, (y_panel, gram)

    z_start = jnp.zeros((N_COLS * CB_DEV, 128, test_cols), jnp.float32)
    z_total, outputs = lax.scan(row_panel, z_start, (tile_values, tile_rows, tile_cols, live_counts))
    y_panels, grams = outputs
    y_sample = y_panels.reshape(N_ROWS * RB_DEV * 128, test_cols)
    z_power = z_total.reshape(N_COLS * CB_DEV * 128, test_cols)
    return y_sample, z_power, grams
```

```python
import jax
import jax.numpy as jnp
from jax import lax
from jax.experimental import pallas as pl
from jax.experimental.pallas import tpu as pltpu
from jax.sharding import Mesh, PartitionSpec as P

RB_DEV = 8
CB_DEV = 4
BLK = 128
PIECES = 64


def split3(v):
    hi = v.astype(jnp.bfloat16)
    rest = v - hi.astype(jnp.float32)
    mid = rest.astype(jnp.bfloat16)
    lo = (rest - mid.astype(jnp.float32)).astype(jnp.bfloat16)
    return hi, mid, lo


def dot3(tile, v, dims):
    hi, mid, lo = split3(v)
    acc = lax.dot_general(tile, lo, dims, preferred_element_type=jnp.float32)
    acc += lax.dot_general(tile, mid, dims, preferred_element_type=jnp.float32)
    return acc + lax.dot_general(tile, hi, dims, preferred_element_type=jnp.float32)


def sample_kernel(rows_ref, cols_ref, live_ref, core_ref, tile_ref, omega_ref, keep_ref, send_ref):
    own = core_ref[0] == 0
    width = omega_ref.shape[1]
    sub = keep_ref.shape[0] // RB_DEV
    part = sub // 4
    keep_ref[...] = jnp.zeros_like(keep_ref)
    send_ref[...] = jnp.zeros_like(send_ref)
    for s in range(tile_ref.shape[0]):

        @pl.when(s < live_ref[0])
        def _():
            base = pl.multiple_of(cols_ref[s] * BLK, BLK)
            prod = dot3(tile_ref[s], omega_ref[pl.ds(base, BLK), :], (((1,), (0,)), ((), ())))
            halves = prod.reshape(4, 2, part, width)
            first = halves[:, 0].reshape(sub, width)
            second = halves[:, 1].reshape(sub, width)
            at = pl.ds(pl.multiple_of(rows_ref[s] * sub, sub), sub)
            keep_ref[at, :] += jnp.where(own, first, second)
            send_ref[at, :] += jnp.where(own, second, first)


def power_kernel(rows_ref, cols_ref, live_ref, core_ref, tile_ref, own_ref, other_ref, *refs):
    out_refs, acc_ref = refs[:-1], refs[-1]
    own = core_ref[0] == 0
    width = own_ref.shape[1]
    sub = own_ref.shape[0] // RB_DEV
    part = sub // 4
    acc_ref[...] = jnp.zeros_like(acc_ref)
    for s in range(tile_ref.shape[0]):

        @pl.when(s < live_ref[0])
        def _():
            at = pl.ds(pl.multiple_of(rows_ref[s] * sub, sub), sub)
            mine, theirs = own_ref[at, :], other_ref[at, :]
            first = jnp.where(own, mine, theirs).reshape(4, part, width)
            second = jnp.where(own, theirs, mine).reshape(4, part, width)
            y_block = jnp.stack([first, second], axis=1).reshape(BLK, width)
            term = dot3(tile_ref[s], y_block, (((0,), (0,)), ((), ())))
            base = pl.multiple_of(cols_ref[s] * BLK, BLK)
            acc_ref[pl.ds(base, BLK), :] += term

    at = 0
    for ref in out_refs:
        ref[...] = acc_ref[at : at + ref.shape[0], :]
        at += ref.shape[0]


def join_kernel(*refs):
    out_ref = refs[-1]
    at = 0
    for ref in refs[:-1]:
        out_ref[at : at + ref.shape[0], :] = ref[...]
        at += ref.shape[0]


VMEM = pl.BlockSpec(memory_space=pltpu.VMEM)
SMEM = pl.BlockSpec(memory_space=pltpu.SMEM)


def make_local(nx, ny, nc):
    def local(tile_values, tile_rows, tile_cols, live_counts, test_block):
        f32 = jnp.float32
        width = test_block.shape[1]
        panel = RB_DEV * BLK
        share = panel // (nx * ny * nc)
        half = panel // nc
        tiles = tile_values[0, 0]
        core = lax.axis_index("core").astype(jnp.int32)[None]
        scalars = (tile_rows[0, 0], tile_cols[0, 0], live_counts[0], core)
        swap = [(0, 1), (1, 0)]

        half_shape = jax.ShapeDtypeStruct((half, width), f32)
        keep, send = pl.pallas_call(
            sample_kernel,
            out_shape=(half_shape, half_shape),
            in_specs=[SMEM] * 4 + [VMEM] * 2,
            out_specs=(VMEM, VMEM),
            name="sample",
        )(*scalars, tiles, test_block)
        part = keep + lax.ppermute(send, "core", swap)
        part = lax.all_to_all(part.reshape(nx, half // nx, width), "x", 0, 0, tiled=True).sum(0)
        part = lax.all_to_all(part.reshape(ny, share, width), "y", 0, 0, tiled=True)
        y_shard = part.sum(0)

        own = jnp.broadcast_to(y_shard[None], (ny, share, width))
        own = lax.all_to_all(own, "y", 0, 0, tiled=True).reshape(ny * share, width)
        own = jnp.broadcast_to(own[None], (nx, ny * share, width))
        own = lax.all_to_all(own, "x", 0, 0, tiled=True).reshape(half, width)
        other = lax.ppermute(own, "core", swap)

        high = lax.Precision.HIGH
        gram = jnp.dot(own.T, own, precision=high, preferred_element_type=f32)
        gram = (gram + jnp.dot(other.T, other, precision=high, preferred_element_type=f32)) / panel

        rows_out = CB_DEV * BLK
        step = rows_out // PIECES
        sizes = [step] * (PIECES - 1) + [step // 2] * 2
        pieces = pl.pallas_call(
            power_kernel,
            out_shape=tuple(jax.ShapeDtypeStruct((n, width), f32) for n in sizes),
            in_specs=[SMEM] * 4 + [VMEM] * 3,
            out_specs=tuple(VMEM for _ in sizes),
            scratch_shapes=[pltpu.VMEM((rows_out, width), f32)],
            name="power",
        )(*scalars, tiles, own, other)
        pieces = lax.psum(pieces, "z")
        z_power = pl.pallas_call(
            join_kernel,
            out_shape=jax.ShapeDtypeStruct((rows_out, width), f32),
            in_specs=[VMEM] * len(sizes),
            out_specs=VMEM,
            name="join",
        )(*pieces)
        return (y_shard, z_power, gram[None])

    return local


def solution(mesh):
    rows, cols = mesh.shape["rows"], mesh.shape["cols"]
    ny, nc = 8, 2
    nx = cols // (ny * nc)
    grid = Mesh(mesh.devices.reshape(rows, nx, ny, nc), ("z", "x", "y", "core"))
    split = ("x", "y", "core")
    return jax.shard_map(
        make_local(nx, ny, nc),
        mesh=grid,
        in_specs=(
            P("z", split, None, None, None),
            P("z", split, None),
            P("z", split, None),
            P("z", split),
            P(split, None),
        ),
        out_specs=(P(("z",) + split, None), P(split, None), P("z", None, None)),
        check_vma=False,
    )
```

```python
import jax
import jax.numpy as jnp
from jax import lax
from jax.experimental import pallas as pl
from jax.experimental.pallas import tpu as pltpu
from jax.sharding import Mesh, PartitionSpec as P

RB_DEV = 8
CB_DEV = 4
BLK = 128
PIECES = 64


def split3(v):
    hi = v.astype(jnp.bfloat16)
    rest = v - hi.astype(jnp.float32)
    mid = rest.astype(jnp.bfloat16)
    lo = (rest - mid.astype(jnp.float32)).astype(jnp.bfloat16)
    return hi, mid, lo


def dot3(tile, v, dims):
    hi, mid, lo = split3(v)
    acc = lax.dot_general(tile, lo, dims, preferred_element_type=jnp.float32)
    acc += lax.dot_general(tile, mid, dims, preferred_element_type=jnp.float32)
    return acc + lax.dot_general(tile, hi, dims, preferred_element_type=jnp.float32)


def sample_kernel(rows_ref, cols_ref, live_ref, core_ref, tile_ref, omega_ref, keep_ref, send_ref):
    own = core_ref[0] == 0
    width = omega_ref.shape[1]
    sub = keep_ref.shape[0] // RB_DEV
    part = sub // 4
    keep_ref[...] = jnp.zeros_like(keep_ref)
    send_ref[...] = jnp.zeros_like(send_ref)
    for s in range(tile_ref.shape[0]):

        @pl.when(s < live_ref[0])
        def _():
            base = pl.multiple_of(cols_ref[s] * BLK, BLK)
            prod = dot3(tile_ref[s], omega_ref[pl.ds(base, BLK), :], (((1,), (0,)), ((), ())))
            halves = prod.reshape(4, 2, part, width)
            first = halves[:, 0].reshape(sub, width)
            second = halves[:, 1].reshape(sub, width)
            at = pl.ds(pl.multiple_of(rows_ref[s] * sub, sub), sub)
            keep_ref[at, :] += jnp.where(own, first, second)
            send_ref[at, :] += jnp.where(own, second, first)


def power_kernel(rows_ref, cols_ref, live_ref, core_ref, tile_ref, own_ref, other_ref, *refs):
    out_refs, acc_ref = refs[:-1], refs[-1]
    own = core_ref[0] == 0
    width = other_ref.shape[1]
    sub = other_ref.shape[0] // RB_DEV
    part = sub // 4
    per = own_ref.shape[1] // sub
    acc_ref[...] = jnp.zeros_like(acc_ref)
    for s in range(tile_ref.shape[0]):

        @pl.when(s < live_ref[0])
        def _():
            at = pl.ds(pl.multiple_of(rows_ref[s] * sub, sub), sub)
            row = rows_ref[s]
            mine = own_ref[row // per, pl.ds(pl.multiple_of(row % per * sub, sub), sub), :]
            theirs = other_ref[at, :]
            first = jnp.where(own, mine, theirs).reshape(4, part, width)
            second = jnp.where(own, theirs, mine).reshape(4, part, width)
            y_block = jnp.stack([first, second], axis=1).reshape(BLK, width)
            term = dot3(tile_ref[s], y_block, (((0,), (0,)), ((), ())))
            base = pl.multiple_of(cols_ref[s] * BLK, BLK)
            acc_ref[pl.ds(base, BLK), :] += term

    at = 0
    for ref in out_refs:
        ref[...] = acc_ref[at : at + ref.shape[0], :]
        at += ref.shape[0]


def finish_kernel(gram_ref, other_ref, *refs):
    pieces, (z_ref, out_ref, sems) = refs[:-3], refs[-3:]
    copies, at = [], 0
    for i, ref in enumerate(pieces):
        copies.append(pltpu.make_async_copy(ref, z_ref.at[at : at + ref.shape[0]], sems.at[i]))
        at += ref.shape[0]
    for copy in copies:
        copy.start()
    v = other_ref[...]
    hi = v.astype(jnp.bfloat16)
    mid = (v - hi.astype(jnp.float32)).astype(jnp.bfloat16)
    dims = (((0,), (0,)), ((), ()))
    acc = lax.dot_general(hi, mid, dims, preferred_element_type=jnp.float32)
    acc += lax.dot_general(mid, hi, dims, preferred_element_type=jnp.float32)
    acc += lax.dot_general(hi, hi, dims, preferred_element_type=jnp.float32)
    out_ref[...] = (gram_ref[...] + acc) * (1.0 / (RB_DEV * BLK))
    for copy in copies:
        copy.wait()


VMEM = pl.BlockSpec(memory_space=pltpu.VMEM)
SMEM = pl.BlockSpec(memory_space=pltpu.SMEM)
ANY = pl.BlockSpec(memory_space=pl.ANY)
PARAMS = pltpu.CompilerParams(vmem_limit_bytes=16 << 20)


def make_local(nx, ny, nc):
    def local(tile_values, tile_rows, tile_cols, live_counts, test_block):
        f32 = jnp.float32
        width = test_block.shape[1]
        panel = RB_DEV * BLK
        share = panel // (nx * ny * nc)
        half = panel // nc
        tiles = tile_values[0, 0]
        core = lax.axis_index("core").astype(jnp.int32)[None]
        scalars = (tile_rows[0, 0], tile_cols[0, 0], live_counts[0], core)
        swap = [(0, 1), (1, 0)]

        half_shape = pltpu.VMEM((half, width), f32)
        keep, send = pl.pallas_call(
            sample_kernel,
            out_shape=(half_shape, half_shape),
            in_specs=[SMEM] * 4 + [VMEM] * 2,
            out_specs=(VMEM, VMEM),
            name="sample",
        )(*scalars, tiles, test_block)
        part = keep + lax.ppermute(send, "core", swap)
        part = lax.all_to_all(part.reshape(nx, half // nx, width), "x", 0, 0, tiled=True).sum(0)
        part = lax.all_to_all(part.reshape(ny, share, width), "y", 0, 0, tiled=True)
        y_shard = part.sum(0)

        own = jnp.broadcast_to(y_shard[None], (ny, share, width))
        own = lax.all_to_all(own, "y", 0, 0, tiled=True).reshape(ny * share, width)
        own = jnp.broadcast_to(own[None], (nx, ny * share, width))
        spread = lax.all_to_all(own, "x", 0, 0, tiled=True)
        own = spread.reshape(half, width)
        other = lax.ppermute(own, "core", swap)

        high = lax.Precision.HIGH
        gram = jnp.dot(own.T, own, precision=high, preferred_element_type=f32)

        rows_out = CB_DEV * BLK
        step = rows_out // PIECES
        sizes = [step] * (PIECES - 1) + [step // 2] * 2
        pieces = pl.pallas_call(
            power_kernel,
            out_shape=tuple(pltpu.HBM((n, width), f32) for n in sizes),
            in_specs=[SMEM] * 4 + [VMEM] * 3,
            out_specs=tuple(VMEM for _ in sizes),
            scratch_shapes=[pltpu.VMEM((rows_out, width), f32)],
            compiler_params=PARAMS,
            name="power",
        )(*scalars, tiles, spread, other)
        pieces = lax.psum(pieces, "z")
        z_power, gram = pl.pallas_call(
            finish_kernel,
            out_shape=(
                jax.ShapeDtypeStruct((rows_out, width), f32),
                jax.ShapeDtypeStruct((width, width), f32),
            ),
            in_specs=[VMEM] * (2 + len(sizes)),
            out_specs=(ANY, VMEM),
            scratch_shapes=[pltpu.SemaphoreType.DMA((len(sizes),))],
            compiler_params=PARAMS,
            name="finish",
        )(gram, other, *[v for v in pieces])
        return (y_shard, z_power, gram[None])

    return local


def solution(mesh):
    rows, cols = mesh.shape["rows"], mesh.shape["cols"]
    ny, nc = 8, 2
    nx = cols // (ny * nc)
    grid = Mesh(mesh.devices.reshape(rows, nx, ny, nc), ("z", "x", "y", "core"))
    split = ("x", "y", "core")
    return jax.shard_map(
        make_local(nx, ny, nc),
        mesh=grid,
        in_specs=(
            P("z", split, None, None, None),
            P("z", split, None),
            P("z", split, None),
            P("z", split),
            P(split, None),
        ),
        out_specs=(P(("z",) + split, None), P(split, None), P("z", None, None)),
        check_vma=False,
    )
```

```python
import jax
import jax.numpy as jnp
from jax import lax
from jax.experimental import pallas as pl
from jax.experimental.pallas import tpu as pltpu
from jax.sharding import Mesh, PartitionSpec as P

RB_DEV = 8
CB_DEV = 4
BLK = 128
PIECES = 64


def tile_dot(tile, v, axis):
    hi = v.astype(jnp.bfloat16)
    mid = (v - hi.astype(jnp.float32)).astype(jnp.bfloat16)
    dims = (((axis,), (0,)), ((), ()))
    return lax.dot_general(
        jnp.concatenate([tile, tile], axis=axis),
        jnp.concatenate([hi, mid], axis=0),
        dims,
        preferred_element_type=jnp.float32,
    )


def sample_kernel(rows_ref, cols_ref, live_ref, core_ref, tile_ref, omega_ref, keep_ref, send_ref):
    own = core_ref[0] == 0
    width = omega_ref.shape[1]
    sub = keep_ref.shape[0] // RB_DEV
    part = sub // 4
    keep_ref[...] = jnp.zeros_like(keep_ref)
    send_ref[...] = jnp.zeros_like(send_ref)
    for s in range(tile_ref.shape[0]):

        @pl.when(s < live_ref[0])
        def _():
            base = pl.multiple_of(cols_ref[s] * BLK, BLK)
            halves = tile_dot(tile_ref[s], omega_ref[pl.ds(base, BLK), :], 1).reshape(4, 2, part, width)
            first = halves[:, 0].reshape(sub, width)
            second = halves[:, 1].reshape(sub, width)
            at = pl.ds(pl.multiple_of(rows_ref[s] * sub, sub), sub)
            keep_ref[at, :] += jnp.where(own, first, second)
            send_ref[at, :] += jnp.where(own, second, first)


def power_kernel(
    rows_ref, cols_ref, live_ref, core_ref, tile_ref, own_ref, other_ref, gram_ref, y_ref, *refs
):
    out_refs, (gram_out, y_out, acc_ref, gram_buf, sems) = refs[:-5], refs[-5:]
    y_copy = pltpu.make_async_copy(y_ref, y_out, sems.at[0])
    y_copy.start()
    chunks, per, sub, width = other_ref.shape
    part = sub // 4
    v = other_ref[...].reshape(per * chunks * sub, width)
    hi = v.astype(jnp.bfloat16)
    mid = (v - hi.astype(jnp.float32)).astype(jnp.bfloat16)
    dims = (((0,), (0,)), ((), ()))
    acc = lax.dot_general(hi, mid, dims, preferred_element_type=jnp.float32)
    acc += lax.dot_general(mid, hi, dims, preferred_element_type=jnp.float32)
    acc += lax.dot_general(hi, hi, dims, preferred_element_type=jnp.float32)
    gram_buf[...] = (gram_ref[...] + acc) * (1.0 / (RB_DEV * BLK))
    gram_copy = pltpu.make_async_copy(gram_buf, gram_out, sems.at[1])
    gram_copy.start()

    own = core_ref[0] == 0
    acc_ref[...] = jnp.zeros_like(acc_ref)
    for s in range(tile_ref.shape[0]):

        @pl.when(s < live_ref[0])
        def _():
            row = rows_ref[s]
            mine, theirs = own_ref[row // per, row % per], other_ref[row // per, row % per]
            first = jnp.where(own, mine, theirs).reshape(4, part, width)
            second = jnp.where(own, theirs, mine).reshape(4, part, width)
            y_block = jnp.stack([first, second], axis=1).reshape(BLK, width)
            base = pl.multiple_of(cols_ref[s] * BLK, BLK)
            acc_ref[pl.ds(base, BLK), :] += tile_dot(tile_ref[s], y_block, 0)

    at = 0
    for ref in out_refs:
        ref[...] = acc_ref[at : at + ref.shape[0], :]
        at += ref.shape[0]
    y_copy.wait()
    gram_copy.wait()


def join_kernel(*refs):
    pieces, (z_ref, sems) = refs[:-2], refs[-2:]
    copies, at = [], 0
    for i, ref in enumerate(pieces):
        copies.append(pltpu.make_async_copy(ref, z_ref.at[at : at + ref.shape[0]], sems.at[i]))
        at += ref.shape[0]
    for copy in copies:
        copy.start()
    for copy in copies:
        copy.wait()


VMEM = pl.BlockSpec(memory_space=pltpu.VMEM)
SMEM = pl.BlockSpec(memory_space=pltpu.SMEM)
ANY = pl.BlockSpec(memory_space=pl.ANY)
PARAMS = pltpu.CompilerParams(vmem_limit_bytes=16 << 20)


def make_local(nx, ny, nc):
    def local(tile_values, tile_rows, tile_cols, live_counts, test_block):
        f32 = jnp.float32
        width = test_block.shape[1]
        panel = RB_DEV * BLK
        share = panel // (nx * ny * nc)
        half = panel // nc
        tiles = tile_values[0, 0]
        core = lax.axis_index("core").astype(jnp.int32)[None]
        scalars = (tile_rows[0, 0], tile_cols[0, 0], live_counts[0], core)
        swap = [(0, 1), (1, 0)]

        half_shape = pltpu.VMEM((half, width), f32)
        keep, send = pl.pallas_call(
            sample_kernel,
            out_shape=(half_shape, half_shape),
            in_specs=[SMEM] * 4 + [VMEM] * 2,
            out_specs=(VMEM, VMEM),
            name="sample",
        )(*scalars, tiles, test_block)
        part = keep + lax.ppermute(send, "core", swap)
        part = lax.all_to_all(part.reshape(nx, half // nx, width), "x", 0, 0, tiled=True).sum(0)
        part = lax.all_to_all(part.reshape(ny, share, width), "y", 0, 0, tiled=True)
        y_shard = part.sum(0)

        own = jnp.broadcast_to(y_shard[None], (ny, share, width))
        own = lax.all_to_all(own, "y", 0, 0, tiled=True)
        sub = half // RB_DEV
        own = own.reshape(RB_DEV // nx, 1, sub, width)
        own = jnp.broadcast_to(own.reshape(1, -1, width), (nx, half // nx, width))
        own = lax.all_to_all(own, "x", 0, 0, tiled=True).reshape(nx, RB_DEV // nx, sub, width)
        other = lax.ppermute(own, "core", swap)

        flat = own.reshape(half, width)
        gram = jnp.dot(flat.T, flat, precision=lax.Precision.HIGH, preferred_element_type=f32)

        rows_out = CB_DEV * BLK
        step = rows_out // PIECES
        sizes = [step] * (PIECES - 1) + [step // 2] * 2
        *pieces, gram, y_out = pl.pallas_call(
            power_kernel,
            out_shape=tuple(jax.ShapeDtypeStruct((n, width), f32) for n in sizes)
            + (
                jax.ShapeDtypeStruct((width, width), f32),
                jax.ShapeDtypeStruct((share, width), f32),
            ),
            in_specs=[SMEM] * 4 + [VMEM] * 5,
            out_specs=tuple(VMEM for _ in sizes) + (ANY, ANY),
            scratch_shapes=[
                pltpu.VMEM((rows_out, width), f32),
                pltpu.VMEM((width, width), f32),
                pltpu.SemaphoreType.DMA((2,)),
            ],
            compiler_params=PARAMS,
            name="power",
        )(*scalars, tiles, own, other, gram, y_shard)
        pieces = lax.psum(pieces, "z")
        z_power = pl.pallas_call(
            join_kernel,
            out_shape=jax.ShapeDtypeStruct((rows_out, width), f32),
            in_specs=[VMEM] * len(sizes),
            out_specs=ANY,
            scratch_shapes=[pltpu.SemaphoreType.DMA((len(sizes),))],
            compiler_params=PARAMS,
            name="join",
        )(*pieces)
        return (y_out, z_power, gram[None])

    return local


def solution(mesh):
    rows, cols = mesh.shape["rows"], mesh.shape["cols"]
    ny, nc = 8, 2
    nx = cols // (ny * nc)
    grid = Mesh(mesh.devices.reshape(rows, nx, ny, nc), ("z", "x", "y", "core"))
    split = ("x", "y", "core")
    return jax.shard_map(
        make_local(nx, ny, nc),
        mesh=grid,
        in_specs=(
            P("z", split, None, None, None),
            P("z", split, None),
            P("z", split, None),
            P("z", split),
            P(split, None),
        ),
        out_specs=(P(("z",) + split, None), P(split, None), P("z", None, None)),
        check_vma=False,
    )
```

```python
import jax
import jax.numpy as jnp
from jax import lax
from jax.experimental import pallas as pl
from jax.experimental.pallas import tpu as pltpu
from jax.sharding import Mesh, PartitionSpec as P

RB_DEV = 8
CB_DEV = 4
BLK = 128
PIECES = 64


def tile_dot(tile, v, axis):
    hi = v.astype(jnp.bfloat16)
    mid = (v - hi.astype(jnp.float32)).astype(jnp.bfloat16)
    dims = (((axis,), (0,)), ((), ()))
    return lax.dot_general(
        jnp.concatenate([tile, tile], axis=axis),
        jnp.concatenate([hi, mid], axis=0),
        dims,
        preferred_element_type=jnp.float32,
    )


def sample_kernel(rows_ref, cols_ref, live_ref, core_ref, tile_ref, omega_ref, keep_ref, send_ref):
    own = core_ref[0] == 0
    width = omega_ref.shape[1]
    sub = keep_ref.shape[0] // RB_DEV
    part = sub // 4
    keep_ref[...] = jnp.zeros_like(keep_ref)
    send_ref[...] = jnp.zeros_like(send_ref)
    for s in range(tile_ref.shape[0]):

        @pl.when(s < live_ref[0])
        def _():
            base = pl.multiple_of(cols_ref[s] * BLK, BLK)
            halves = tile_dot(tile_ref[s], omega_ref[pl.ds(base, BLK), :], 1).reshape(2, 2, 2, part, width)
            row = rows_ref[s]
            for odd in range(2):
                first = halves[:, odd, 0].reshape(2 * part, width)
                second = halves[:, odd, 1].reshape(2 * part, width)
                at = (row // 2 * 2 + odd) * sub + row % 2 * (2 * part)
                at = pl.ds(pl.multiple_of(at, 2 * part), 2 * part)
                keep_ref[at, :] += jnp.where(own, first, second)
                send_ref[at, :] += jnp.where(own, second, first)


def power_kernel(
    rows_ref, cols_ref, live_ref, core_ref, tile_ref, own_ref, other_ref, gram_ref, y_ref, *refs
):
    out_refs, (gram_out, y_out, acc_ref, gram_buf, sems) = refs[:-5], refs[-5:]
    y_copy = pltpu.make_async_copy(y_ref, y_out, sems.at[0])
    y_copy.start()
    places, sub, width = other_ref.shape
    part = sub // 4
    v = other_ref[...].reshape(places * sub, width)
    hi = v.astype(jnp.bfloat16)
    mid = (v - hi.astype(jnp.float32)).astype(jnp.bfloat16)
    dims = (((0,), (0,)), ((), ()))
    acc = lax.dot_general(hi, mid, dims, preferred_element_type=jnp.float32)
    acc += lax.dot_general(mid, hi, dims, preferred_element_type=jnp.float32)
    acc += lax.dot_general(hi, hi, dims, preferred_element_type=jnp.float32)
    gram_buf[...] = (gram_ref[...] + acc) * (1.0 / (RB_DEV * BLK))
    gram_copy = pltpu.make_async_copy(gram_buf, gram_out, sems.at[1])
    gram_copy.start()

    own = core_ref[0] == 0
    acc_ref[...] = jnp.zeros_like(acc_ref)
    for s in range(tile_ref.shape[0]):

        @pl.when(s < live_ref[0])
        def _():
            row = rows_ref[s]
            at = pl.ds(pl.multiple_of(row % 2 * (2 * part), 2 * part), 2 * part)
            parts = []
            for odd in range(2):
                mine, theirs = own_ref[row // 2 * 2 + odd, at, :], other_ref[row // 2 * 2 + odd, at, :]
                parts.append(jnp.where(own, mine, theirs).reshape(2, part, width))
                parts.append(jnp.where(own, theirs, mine).reshape(2, part, width))
            y_block = jnp.stack(parts, axis=1).reshape(BLK, width)
            base = pl.multiple_of(cols_ref[s] * BLK, BLK)
            acc_ref[pl.ds(base, BLK), :] += tile_dot(tile_ref[s], y_block, 0)

    at = 0
    for ref in out_refs:
        ref[...] = acc_ref[at : at + ref.shape[0], :]
        at += ref.shape[0]
    y_copy.wait()
    gram_copy.wait()


def join_kernel(*refs):
    pieces, (z_ref, sems) = refs[:-2], refs[-2:]
    copies, at = [], 0
    for i, ref in enumerate(pieces):
        copies.append(pltpu.make_async_copy(ref, z_ref.at[at : at + ref.shape[0]], sems.at[i]))
        at += ref.shape[0]
    for copy in copies:
        copy.start()
    for copy in copies:
        copy.wait()


VMEM = pl.BlockSpec(memory_space=pltpu.VMEM)
SMEM = pl.BlockSpec(memory_space=pltpu.SMEM)
ANY = pl.BlockSpec(memory_space=pl.ANY)
PARAMS = pltpu.CompilerParams(vmem_limit_bytes=16 << 20)


def make_local(nx, ny, nc):
    def local(tile_values, tile_rows, tile_cols, live_counts, test_block):
        f32 = jnp.float32
        width = test_block.shape[1]
        panel = RB_DEV * BLK
        share = panel // (nx * ny * nc)
        half = panel // nc
        tiles = tile_values[0, 0]
        core = lax.axis_index("core").astype(jnp.int32)[None]
        scalars = (tile_rows[0, 0], tile_cols[0, 0], live_counts[0], core)
        swap = [(0, 1), (1, 0)]

        half_shape = pltpu.VMEM((half, width), f32)
        keep, send = pl.pallas_call(
            sample_kernel,
            out_shape=(half_shape, half_shape),
            in_specs=[SMEM] * 4 + [VMEM] * 2,
            out_specs=(VMEM, VMEM),
            name="sample",
        )(*scalars, tiles, test_block)
        part = keep + lax.ppermute(send, "core", swap)
        near, far = nx * 2, ny // 2
        part = part.reshape(near, half // near, width)
        part = lax.all_to_all(part, ("x", "odd"), 0, 0, tiled=True).sum(0)
        part = lax.all_to_all(part.reshape(far, share, width), "pair", 0, 0, tiled=True)
        y_shard = part.sum(0)

        own = jnp.broadcast_to(y_shard[None], (far, share, width))
        own = lax.all_to_all(own, "pair", 0, 0, tiled=True).reshape(1, far * share, width)
        own = jnp.broadcast_to(own, (near, far * share, width))
        own = lax.all_to_all(own, ("x", "odd"), 0, 0, tiled=True)
        other = lax.ppermute(own, "core", swap)

        flat = own.reshape(half, width)
        gram = jnp.dot(flat.T, flat, precision=lax.Precision.HIGH, preferred_element_type=f32)

        rows_out = CB_DEV * BLK
        step = rows_out // PIECES
        sizes = [step] * (PIECES - 1) + [step // 2] * 2
        *pieces, gram, y_out = pl.pallas_call(
            power_kernel,
            out_shape=tuple(jax.ShapeDtypeStruct((n, width), f32) for n in sizes)
            + (
                jax.ShapeDtypeStruct((width, width), f32),
                jax.ShapeDtypeStruct((share, width), f32),
            ),
            in_specs=[SMEM] * 4 + [VMEM] * 5,
            out_specs=tuple(VMEM for _ in sizes) + (ANY, ANY),
            scratch_shapes=[
                pltpu.VMEM((rows_out, width), f32),
                pltpu.VMEM((width, width), f32),
                pltpu.SemaphoreType.DMA((2,)),
            ],
            compiler_params=PARAMS,
            name="power",
        )(*scalars, tiles, own, other, gram, y_shard)
        pieces = lax.psum(pieces, "z")
        z_power = pl.pallas_call(
            join_kernel,
            out_shape=jax.ShapeDtypeStruct((rows_out, width), f32),
            in_specs=[VMEM] * len(sizes),
            out_specs=ANY,
            scratch_shapes=[pltpu.SemaphoreType.DMA((len(sizes),))],
            compiler_params=PARAMS,
            name="join",
        )(*pieces)
        return (y_out, z_power, gram[None])

    return local


def solution(mesh):
    rows, cols = mesh.shape["rows"], mesh.shape["cols"]
    ny, nc = 8, 2
    nx = cols // (ny * nc)
    grid = Mesh(mesh.devices.reshape(rows, nx, ny // 2, 2, nc), ("z", "x", "pair", "odd", "core"))
    split = ("x", "pair", "odd", "core")
    return jax.shard_map(
        make_local(nx, ny, nc),
        mesh=grid,
        in_specs=(
            P("z", split, None, None, None),
            P("z", split, None),
            P("z", split, None),
            P("z", split),
            P(split, None),
        ),
        out_specs=(P(("z",) + split, None), P(split, None), P("z", None, None)),
        check_vma=False,
    )
```

```python
import jax
import jax.numpy as jnp
from jax import lax
from jax.experimental import pallas as pl
from jax.experimental.pallas import tpu as pltpu
from jax.sharding import Mesh, PartitionSpec as P

RB_DEV = 8
CB_DEV = 4
BLK = 128
PIECES = 64


def tile_dot(tile, v, axis):
    hi = v.astype(jnp.bfloat16)
    mid = (v - hi.astype(jnp.float32)).astype(jnp.bfloat16)
    dims = (((axis,), (0,)), ((), ()))
    return lax.dot_general(
        jnp.concatenate([tile, tile], axis=axis),
        jnp.concatenate([hi, mid], axis=0),
        dims,
        preferred_element_type=jnp.float32,
    )


def sample_kernel(rows_ref, cols_ref, live_ref, core_ref, tile_ref, omega_ref, keep_ref, send_ref):
    own = core_ref[0] == 0
    width = omega_ref.shape[1]
    sub = keep_ref.shape[0] // RB_DEV
    part = sub // 4
    keep_ref[...] = jnp.zeros_like(keep_ref)
    send_ref[...] = jnp.zeros_like(send_ref)
    for s in range(tile_ref.shape[0]):

        @pl.when(s < live_ref[0])
        def _():
            base = pl.multiple_of(cols_ref[s] * BLK, BLK)
            halves = tile_dot(tile_ref[s], omega_ref[pl.ds(base, BLK), :], 1).reshape(2, 2, 2, part, width)
            row = rows_ref[s]
            for odd in range(2):
                first = halves[:, odd, 0].reshape(2 * part, width)
                second = halves[:, odd, 1].reshape(2 * part, width)
                at = (row // 2 * 2 + odd) * sub + row % 2 * (2 * part)
                at = pl.ds(pl.multiple_of(at, 2 * part), 2 * part)
                keep_ref[at, :] += jnp.where(own, first, second)
                send_ref[at, :] += jnp.where(own, second, first)


def power_kernel(
    rows_ref, cols_ref, live_ref, core_ref, tile_ref, own_ref, other_ref, gram_ref, y_ref, place_ref, *refs
):
    out_refs, (gram_out, y_out, acc_ref, gram_buf, sems) = refs[:-5], refs[-5:]
    share = y_out.shape[0]
    y_at = pl.ds(pl.multiple_of(place_ref[0] * share, share), share)
    y_copy = pltpu.make_async_copy(y_ref.at[y_at], y_out, sems.at[0])
    y_copy.start()
    places, sub, width = other_ref.shape
    part = sub // 4
    v = other_ref[...].reshape(places * sub, width)
    hi = v.astype(jnp.bfloat16)
    mid = (v - hi.astype(jnp.float32)).astype(jnp.bfloat16)
    dims = (((0,), (0,)), ((), ()))
    acc = lax.dot_general(hi, mid, dims, preferred_element_type=jnp.float32)
    acc += lax.dot_general(mid, hi, dims, preferred_element_type=jnp.float32)
    acc += lax.dot_general(hi, hi, dims, preferred_element_type=jnp.float32)
    gram_buf[...] = (gram_ref[...] + acc) * (1.0 / (RB_DEV * BLK))
    gram_copy = pltpu.make_async_copy(gram_buf, gram_out, sems.at[1])
    gram_copy.start()

    own = core_ref[0] == 0
    acc_ref[...] = jnp.zeros_like(acc_ref)
    for s in range(tile_ref.shape[0]):

        @pl.when(s < live_ref[0])
        def _():
            row = rows_ref[s]
            at = pl.ds(pl.multiple_of(row % 2 * (2 * part), 2 * part), 2 * part)
            parts = []
            for odd in range(2):
                mine, theirs = own_ref[row // 2 * 2 + odd, at, :], other_ref[row // 2 * 2 + odd, at, :]
                parts.append(jnp.where(own, mine, theirs).reshape(2, part, width))
                parts.append(jnp.where(own, theirs, mine).reshape(2, part, width))
            y_block = jnp.stack(parts, axis=1).reshape(BLK, width)
            base = pl.multiple_of(cols_ref[s] * BLK, BLK)
            acc_ref[pl.ds(base, BLK), :] += tile_dot(tile_ref[s], y_block, 0)

    at = 0
    for ref in out_refs:
        ref[...] = acc_ref[at : at + ref.shape[0], :]
        at += ref.shape[0]
    y_copy.wait()
    gram_copy.wait()


def join_kernel(*refs):
    pieces, (z_ref, sems) = refs[:-2], refs[-2:]
    copies, at = [], 0
    for i, ref in enumerate(pieces):
        copies.append(pltpu.make_async_copy(ref, z_ref.at[at : at + ref.shape[0]], sems.at[i]))
        at += ref.shape[0]
    for copy in copies:
        copy.start()
    for copy in copies:
        copy.wait()


VMEM = pl.BlockSpec(memory_space=pltpu.VMEM)
SMEM = pl.BlockSpec(memory_space=pltpu.SMEM)
ANY = pl.BlockSpec(memory_space=pl.ANY)
PARAMS = pltpu.CompilerParams(vmem_limit_bytes=16 << 20)


def make_local(nx, ny, nc):
    def local(tile_values, tile_rows, tile_cols, live_counts, test_block):
        f32 = jnp.float32
        width = test_block.shape[1]
        panel = RB_DEV * BLK
        share = panel // (nx * ny * nc)
        half = panel // nc
        tiles = tile_values[0, 0]
        core = lax.axis_index("core").astype(jnp.int32)[None]
        place = lax.axis_index("pair").astype(jnp.int32)[None]
        scalars = (tile_rows[0, 0], tile_cols[0, 0], live_counts[0], core)
        swap = [(0, 1), (1, 0)]

        half_shape = pltpu.VMEM((half, width), f32)
        keep, send = pl.pallas_call(
            sample_kernel,
            out_shape=(half_shape, half_shape),
            in_specs=[SMEM] * 4 + [VMEM] * 2,
            out_specs=(VMEM, VMEM),
            name="sample",
        )(*scalars, tiles, test_block)
        part = keep + lax.ppermute(send, "core", swap)
        near, far = nx * 2, ny // 2
        part = part.reshape(near, half // near, width)
        part = lax.all_to_all(part, ("x", "odd"), 0, 0, tiled=True).sum(0)
        chunk = lax.all_gather(part, "pair", axis=0, tiled=False).sum(0)
        own = jnp.broadcast_to(chunk[None], (near, far * share, width))
        own = lax.all_to_all(own, ("x", "odd"), 0, 0, tiled=True)
        other = lax.ppermute(own, "core", swap)

        flat = own.reshape(half, width)
        gram = jnp.dot(flat.T, flat, precision=lax.Precision.HIGH, preferred_element_type=f32)

        rows_out = CB_DEV * BLK
        step = rows_out // PIECES
        sizes = [step] * (PIECES - 1) + [step // 2] * 2
        *pieces, gram, y_out = pl.pallas_call(
            power_kernel,
            out_shape=tuple(jax.ShapeDtypeStruct((n, width), f32) for n in sizes)
            + (
                jax.ShapeDtypeStruct((width, width), f32),
                jax.ShapeDtypeStruct((share, width), f32),
            ),
            in_specs=[SMEM] * 4 + [VMEM] * 5 + [SMEM],
            out_specs=tuple(VMEM for _ in sizes) + (ANY, ANY),
            scratch_shapes=[
                pltpu.VMEM((rows_out, width), f32),
                pltpu.VMEM((width, width), f32),
                pltpu.SemaphoreType.DMA((2,)),
            ],
            compiler_params=PARAMS,
            name="power",
        )(*scalars, tiles, own, other, gram, chunk, place)
        pieces = lax.psum(pieces, "z")
        z_power = pl.pallas_call(
            join_kernel,
            out_shape=jax.ShapeDtypeStruct((rows_out, width), f32),
            in_specs=[VMEM] * len(sizes),
            out_specs=ANY,
            scratch_shapes=[pltpu.SemaphoreType.DMA((len(sizes),))],
            compiler_params=PARAMS,
            name="join",
        )(*pieces)
        return (y_out, z_power, gram[None])

    return local


def solution(mesh):
    rows, cols = mesh.shape["rows"], mesh.shape["cols"]
    ny, nc = 8, 2
    nx = cols // (ny * nc)
    grid = Mesh(mesh.devices.reshape(rows, nx, ny // 2, 2, nc), ("z", "x", "pair", "odd", "core"))
    split = ("x", "pair", "odd", "core")
    return jax.shard_map(
        make_local(nx, ny, nc),
        mesh=grid,
        in_specs=(
            P("z", split, None, None, None),
            P("z", split, None),
            P("z", split, None),
            P("z", split),
            P(split, None),
        ),
        out_specs=(P(("z",) + split, None), P(split, None), P("z", None, None)),
        check_vma=False,
    )
```

```python
import jax
import jax.numpy as jnp
from jax import lax
from jax.experimental import pallas as pl
from jax.experimental.pallas import tpu as pltpu
from jax.sharding import Mesh, PartitionSpec as P

RB_DEV = 8
CB_DEV = 4
BLK = 128
PIECES = 64


def tile_dot(tile, v, axis):
    hi = v.astype(jnp.bfloat16)
    mid = (v - hi.astype(jnp.float32)).astype(jnp.bfloat16)
    dims = (((axis,), (0,)), ((), ()))
    return lax.dot_general(
        jnp.concatenate([tile, tile], axis=axis),
        jnp.concatenate([hi, mid], axis=0),
        dims,
        preferred_element_type=jnp.float32,
    )


def sample_kernel(rows_ref, cols_ref, live_ref, core_ref, tile_ref, omega_ref, keep_ref, send_ref):
    own = core_ref[0] == 0
    width = omega_ref.shape[1]
    sub = keep_ref.shape[0] // RB_DEV
    part = sub // 4
    keep_ref[...] = jnp.zeros_like(keep_ref)
    send_ref[...] = jnp.zeros_like(send_ref)
    for s in range(tile_ref.shape[0]):

        @pl.when(s < live_ref[0])
        def _():
            base = pl.multiple_of(cols_ref[s] * BLK, BLK)
            halves = tile_dot(tile_ref[s], omega_ref[pl.ds(base, BLK), :], 1).reshape(2, 2, 2, part, width)
            row = rows_ref[s]
            for odd in range(2):
                first = halves[:, odd, 0].reshape(2 * part, width)
                second = halves[:, odd, 1].reshape(2 * part, width)
                at = (row // 2 * 2 + odd) * sub + row % 2 * (2 * part)
                at = pl.ds(pl.multiple_of(at, 2 * part), 2 * part)
                keep_ref[at, :] += jnp.where(own, first, second)
                send_ref[at, :] += jnp.where(own, second, first)


def power_kernel(
    table_ref, tile_ref, own_ref, other_ref, gram_ref, y_ref, *refs
):
    slots = tile_ref.shape[0]
    out_refs, (gram_out, y_out, acc_ref, gram_buf, sems) = refs[:-5], refs[-5:]
    share = y_out.shape[0]
    y_at = pl.ds(pl.multiple_of(table_ref[2 * slots + 2] * share, share), share)
    y_copy = pltpu.make_async_copy(y_ref.at[y_at], y_out, sems.at[0])
    y_copy.start()
    places, sub, width = other_ref.shape
    part = sub // 4
    v = other_ref[...].reshape(places * sub, width)
    hi = v.astype(jnp.bfloat16)
    mid = (v - hi.astype(jnp.float32)).astype(jnp.bfloat16)
    dims = (((0,), (0,)), ((), ()))
    acc = lax.dot_general(hi, mid, dims, preferred_element_type=jnp.float32)
    acc += lax.dot_general(mid, hi, dims, preferred_element_type=jnp.float32)
    acc += lax.dot_general(hi, hi, dims, preferred_element_type=jnp.float32)
    gram_buf[...] = (gram_ref[...] + acc) * (1.0 / (RB_DEV * BLK))
    gram_copy = pltpu.make_async_copy(gram_buf, gram_out, sems.at[1])
    gram_copy.start()

    own = table_ref[2 * slots + 1] == 0
    acc_ref[...] = jnp.zeros_like(acc_ref)
    for s in range(slots):

        @pl.when(s < table_ref[2 * slots])
        def _():
            row = table_ref[s]
            at = pl.ds(pl.multiple_of(row % 2 * (2 * part), 2 * part), 2 * part)
            parts = []
            for odd in range(2):
                mine, theirs = own_ref[row // 2 * 2 + odd, at, :], other_ref[row // 2 * 2 + odd, at, :]
                parts.append(jnp.where(own, mine, theirs).reshape(2, part, width))
                parts.append(jnp.where(own, theirs, mine).reshape(2, part, width))
            y_block = jnp.stack(parts, axis=1).reshape(BLK, width)
            base = pl.multiple_of(table_ref[slots + s] * BLK, BLK)
            acc_ref[pl.ds(base, BLK), :] += tile_dot(tile_ref[s], y_block, 0)

    at = 0
    for ref in out_refs:
        ref[...] = acc_ref[at : at + ref.shape[0], :]
        at += ref.shape[0]
    y_copy.wait()
    gram_copy.wait()


def join_kernel(*refs):
    pieces, (z_ref, sems) = refs[:-2], refs[-2:]
    copies, at = [], 0
    for i, ref in enumerate(pieces):
        copies.append(pltpu.make_async_copy(ref, z_ref.at[at : at + ref.shape[0]], sems.at[i]))
        at += ref.shape[0]
    for copy in copies:
        copy.start()
    for copy in copies:
        copy.wait()


VMEM = pl.BlockSpec(memory_space=pltpu.VMEM)
SMEM = pl.BlockSpec(memory_space=pltpu.SMEM)
ANY = pl.BlockSpec(memory_space=pl.ANY)
PARAMS = pltpu.CompilerParams(vmem_limit_bytes=16 << 20)


def make_local(nx, ny, nc):
    def local(tile_values, tile_rows, tile_cols, live_counts, test_block):
        f32 = jnp.float32
        width = test_block.shape[1]
        panel = RB_DEV * BLK
        share = panel // (nx * ny * nc)
        half = panel // nc
        tiles = tile_values[0, 0]
        core = lax.axis_index("core").astype(jnp.int32)[None]
        place = lax.axis_index("pair").astype(jnp.int32)[None]
        scalars = (tile_rows[0, 0], tile_cols[0, 0], live_counts[0], core)
        swap = [(0, 1), (1, 0)]

        half_shape = pltpu.VMEM((half, width), f32)
        keep, send = pl.pallas_call(
            sample_kernel,
            out_shape=(half_shape, half_shape),
            in_specs=[SMEM] * 4 + [VMEM] * 2,
            out_specs=(VMEM, VMEM),
            name="sample",
        )(*scalars, tiles, test_block)
        part = keep + lax.ppermute(send, "core", swap)
        near, far = nx * 2, ny // 2
        part = part.reshape(near, half // near, width)
        part = lax.all_to_all(part, ("x", "odd"), 0, 0, tiled=True).sum(0)
        chunk = lax.all_gather(part, "pair", axis=0, tiled=False).sum(0)
        own = jnp.broadcast_to(chunk[None], (near, far * share, width))
        own = lax.all_to_all(own, ("x", "odd"), 0, 0, tiled=True)
        other = lax.ppermute(own, "core", swap)

        flat = own.reshape(half, width)
        gram = jnp.dot(flat.T, flat, precision=lax.Precision.HIGH, preferred_element_type=f32)

        table = jnp.concatenate(scalars + (place,))
        rows_out = CB_DEV * BLK
        step = rows_out // PIECES
        sizes = [step] * (PIECES - 1) + [step // 2] * 2
        *pieces, gram, y_out = pl.pallas_call(
            power_kernel,
            out_shape=tuple(jax.ShapeDtypeStruct((n, width), f32) for n in sizes)
            + (
                jax.ShapeDtypeStruct((width, width), f32),
                jax.ShapeDtypeStruct((share, width), f32),
            ),
            in_specs=[SMEM] + [VMEM] * 5,
            out_specs=tuple(VMEM for _ in sizes) + (ANY, ANY),
            scratch_shapes=[
                pltpu.VMEM((rows_out, width), f32),
                pltpu.VMEM((width, width), f32),
                pltpu.SemaphoreType.DMA((2,)),
            ],
            compiler_params=PARAMS,
            name="power",
        )(table, tiles, own, other, gram, chunk)
        pieces = lax.psum(pieces, "z")
        z_power = pl.pallas_call(
            join_kernel,
            out_shape=jax.ShapeDtypeStruct((rows_out, width), f32),
            in_specs=[VMEM] * len(sizes),
            out_specs=ANY,
            scratch_shapes=[pltpu.SemaphoreType.DMA((len(sizes),))],
            compiler_params=PARAMS,
            name="join",
        )(*pieces)
        return (y_out, z_power, gram[None])

    return local


def solution(mesh):
    rows, cols = mesh.shape["rows"], mesh.shape["cols"]
    ny, nc = 8, 2
    nx = cols // (ny * nc)
    grid = Mesh(mesh.devices.reshape(rows, nx, ny // 2, 2, nc), ("z", "x", "pair", "odd", "core"))
    split = ("x", "pair", "odd", "core")
    return jax.shard_map(
        make_local(nx, ny, nc),
        mesh=grid,
        in_specs=(
            P("z", split, None, None, None),
            P("z", split, None),
            P("z", split, None),
            P("z", split),
            P(split, None),
        ),
        out_specs=(P(("z",) + split, None), P(split, None), P("z", None, None)),
        check_vma=False,
    )
```

```python
import jax
import jax.numpy as jnp
from jax import lax
from jax.experimental import pallas as pl
from jax.experimental.pallas import tpu as pltpu
from jax.sharding import Mesh, PartitionSpec as P

RB_DEV = 8
CB_DEV = 4
BLK = 128
PIECES = 64


def tile_dot(tile, v, axis):
    hi = v.astype(jnp.bfloat16)
    mid = (v - hi.astype(jnp.float32)).astype(jnp.bfloat16)
    dims = (((axis,), (0,)), ((), ()))
    return lax.dot_general(
        jnp.concatenate([tile, tile], axis=axis),
        jnp.concatenate([hi, mid], axis=0),
        dims,
        preferred_element_type=jnp.float32,
    )


def sample_kernel(rows_ref, cols_ref, live_ref, core_ref, tile_ref, omega_ref, keep_ref, send_ref):
    own = core_ref[0] == 0
    width = omega_ref.shape[1]
    sub = keep_ref.shape[0] // RB_DEV
    part = sub // 4
    keep_ref[...] = jnp.zeros_like(keep_ref)
    send_ref[...] = jnp.zeros_like(send_ref)
    for s in range(tile_ref.shape[0]):

        @pl.when(s < live_ref[0])
        def _():
            base = pl.multiple_of(cols_ref[s] * BLK, BLK)
            halves = tile_dot(tile_ref[s], omega_ref[pl.ds(base, BLK), :], 1).reshape(2, 2, 2, part, width)
            row = rows_ref[s]
            for odd in range(2):
                first = halves[:, odd, 0].reshape(2 * part, width)
                second = halves[:, odd, 1].reshape(2 * part, width)
                at = (odd * (RB_DEV // 2) + row // 2) * sub + row % 2 * (2 * part)
                at = pl.ds(pl.multiple_of(at, 2 * part), 2 * part)
                keep_ref[at, :] += jnp.where(own, first, second)
                send_ref[at, :] += jnp.where(own, second, first)


def power_kernel(
    table_ref, tile_ref, own_ref, other_ref, gram_ref, y_ref, *refs
):
    slots = tile_ref.shape[0]
    out_refs, (gram_out, y_out, acc_ref, gram_buf, sems) = refs[:-5], refs[-5:]
    share = y_out.shape[0]
    y_at = pl.ds(pl.multiple_of(table_ref[2 * slots + 2] * share, share), share)
    y_copy = pltpu.make_async_copy(y_ref.at[y_at], y_out, sems.at[0])
    y_copy.start()
    places, sub, width = other_ref.shape
    part = sub // 4
    v = other_ref[...].reshape(places * sub, width)
    hi = v.astype(jnp.bfloat16)
    mid = (v - hi.astype(jnp.float32)).astype(jnp.bfloat16)
    dims = (((0,), (0,)), ((), ()))
    acc = lax.dot_general(hi, mid, dims, preferred_element_type=jnp.float32)
    acc += lax.dot_general(mid, hi, dims, preferred_element_type=jnp.float32)
    acc += lax.dot_general(hi, hi, dims, preferred_element_type=jnp.float32)
    gram_buf[...] = (gram_ref[...] + acc) * (1.0 / (RB_DEV * BLK))
    gram_copy = pltpu.make_async_copy(gram_buf, gram_out, sems.at[1])
    gram_copy.start()

    own = table_ref[2 * slots + 1] == 0
    acc_ref[...] = jnp.zeros_like(acc_ref)
    for s in range(slots):

        @pl.when(s < table_ref[2 * slots])
        def _():
            row = table_ref[s]
            at = pl.ds(pl.multiple_of(row % 2 * (2 * part), 2 * part), 2 * part)
            parts = []
            for odd in range(2):
                mine, theirs = own_ref[odd * (RB_DEV // 2) + row // 2, at, :], other_ref[odd * (RB_DEV // 2) + row // 2, at, :]
                parts.append(jnp.where(own, mine, theirs).reshape(2, part, width))
                parts.append(jnp.where(own, theirs, mine).reshape(2, part, width))
            y_block = jnp.stack(parts, axis=1).reshape(BLK, width)
            base = pl.multiple_of(table_ref[slots + s] * BLK, BLK)
            acc_ref[pl.ds(base, BLK), :] += tile_dot(tile_ref[s], y_block, 0)

    at = 0
    for ref in out_refs:
        ref[...] = acc_ref[at : at + ref.shape[0], :]
        at += ref.shape[0]
    y_copy.wait()
    gram_copy.wait()


def join_kernel(*refs):
    pieces, (z_ref, sems) = refs[:-2], refs[-2:]
    copies, at = [], 0
    for i, ref in enumerate(pieces):
        copies.append(pltpu.make_async_copy(ref, z_ref.at[at : at + ref.shape[0]], sems.at[i]))
        at += ref.shape[0]
    for copy in copies:
        copy.start()
    for copy in copies:
        copy.wait()


VMEM = pl.BlockSpec(memory_space=pltpu.VMEM)
SMEM = pl.BlockSpec(memory_space=pltpu.SMEM)
ANY = pl.BlockSpec(memory_space=pl.ANY)
PARAMS = pltpu.CompilerParams(vmem_limit_bytes=16 << 20)


def make_local(nx, ny, nc):
    def local(tile_values, tile_rows, tile_cols, live_counts, test_block):
        f32 = jnp.float32
        width = test_block.shape[1]
        panel = RB_DEV * BLK
        share = panel // (nx * ny * nc)
        half = panel // nc
        tiles = tile_values[0, 0]
        core = lax.axis_index("core").astype(jnp.int32)[None]
        place = lax.axis_index("pair").astype(jnp.int32)[None]
        scalars = (tile_rows[0, 0], tile_cols[0, 0], live_counts[0], core)
        swap = [(0, 1), (1, 0)]

        half_shape = pltpu.VMEM((half, width), f32)
        keep, send = pl.pallas_call(
            sample_kernel,
            out_shape=(half_shape, half_shape),
            in_specs=[SMEM] * 4 + [VMEM] * 2,
            out_specs=(VMEM, VMEM),
            name="sample",
        )(*scalars, tiles, test_block)
        part = keep + lax.ppermute(send, "core", swap)
        near, far = nx * 2, ny // 2
        part = part.reshape(near, half // near, width)
        part = lax.all_to_all(part, ("odd", "x"), 0, 0, tiled=True).sum(0)
        chunk = lax.all_gather(part, "pair", axis=0, tiled=False).sum(0)
        own = jnp.broadcast_to(chunk[None], (near, far * share, width))
        own = lax.all_to_all(own, ("odd", "x"), 0, 0, tiled=True)
        other = lax.ppermute(own, "core", swap)

        flat = own.reshape(half, width)
        gram = jnp.dot(flat.T, flat, precision=lax.Precision.HIGH, preferred_element_type=f32)

        table = jnp.concatenate(scalars + (place,))
        rows_out = CB_DEV * BLK
        step = rows_out // PIECES
        sizes = [step] * (PIECES - 1) + [step // 2] * 2
        *pieces, gram, y_out = pl.pallas_call(
            power_kernel,
            out_shape=tuple(jax.ShapeDtypeStruct((n, width), f32) for n in sizes)
            + (
                jax.ShapeDtypeStruct((width, width), f32),
                jax.ShapeDtypeStruct((share, width), f32),
            ),
            in_specs=[SMEM] + [VMEM] * 5,
            out_specs=tuple(VMEM for _ in sizes) + (ANY, ANY),
            scratch_shapes=[
                pltpu.VMEM((rows_out, width), f32),
                pltpu.VMEM((width, width), f32),
                pltpu.SemaphoreType.DMA((2,)),
            ],
            compiler_params=PARAMS,
            name="power",
        )(table, tiles, own, other, gram, chunk)
        pieces = lax.psum(pieces, "z")
        z_power = pl.pallas_call(
            join_kernel,
            out_shape=jax.ShapeDtypeStruct((rows_out, width), f32),
            in_specs=[VMEM] * len(sizes),
            out_specs=ANY,
            scratch_shapes=[pltpu.SemaphoreType.DMA((len(sizes),))],
            compiler_params=PARAMS,
            name="join",
        )(*pieces)
        return (y_out, z_power, gram[None])

    return local


def solution(mesh):
    rows, cols = mesh.shape["rows"], mesh.shape["cols"]
    ny, nc = 8, 2
    nx = cols // (ny * nc)
    grid = Mesh(mesh.devices.reshape(rows, nx, ny // 2, 2, nc), ("z", "x", "pair", "odd", "core"))
    split = ("x", "pair", "odd", "core")
    return jax.shard_map(
        make_local(nx, ny, nc),
        mesh=grid,
        in_specs=(
            P("z", split, None, None, None),
            P("z", split, None),
            P("z", split, None),
            P("z", split),
            P(split, None),
        ),
        out_specs=(P(("z",) + split, None), P(split, None), P("z", None, None)),
        check_vma=False,
    )
```

```python
import jax
import jax.numpy as jnp
from jax import lax
from jax.experimental import pallas as pl
from jax.experimental.pallas import tpu as pltpu
from jax.sharding import Mesh, PartitionSpec as P

RB_DEV = 8
CB_DEV = 4
BLK = 128
PIECES = 64


def tile_dot(tile, v, axis):
    hi = v.astype(jnp.bfloat16)
    mid = (v - hi.astype(jnp.float32)).astype(jnp.bfloat16)
    dims = (((axis,), (0,)), ((), ()))
    return lax.dot_general(
        jnp.concatenate([tile, tile], axis=axis),
        jnp.concatenate([hi, mid], axis=0),
        dims,
        preferred_element_type=jnp.float32,
    )


def sample_kernel(rows_ref, cols_ref, live_ref, core_ref, tile_ref, omega_ref, out_ref):
    lower = core_ref[0] == 0
    width = omega_ref.shape[1]
    sub = out_ref.shape[0] // RB_DEV
    part = sub // 4
    out_ref[...] = jnp.zeros_like(out_ref)
    for s in range(tile_ref.shape[0]):

        @pl.when(s < live_ref[0])
        def _():
            base = pl.multiple_of(cols_ref[s] * BLK, BLK)
            tile = tile_ref[s].reshape(4, 2, part, BLK)
            tile = jnp.where(lower, tile[:, 0], tile[:, 1]).reshape(sub, BLK)
            prod = tile_dot(tile, omega_ref[pl.ds(base, BLK), :], 1).reshape(2, 2, part, width)
            row = rows_ref[s]
            for odd in range(2):
                at = (odd * (RB_DEV // 2) + row // 2) * sub + row % 2 * (2 * part)
                at = pl.ds(pl.multiple_of(at, 2 * part), 2 * part)
                out_ref[at, :] += prod[:, odd].reshape(2 * part, width)


def power_kernel(
    table_ref, tile_ref, own_ref, other_ref, gram_ref, y_ref, *refs
):
    slots = tile_ref.shape[0]
    out_refs, (gram_out, y_out, acc_ref, gram_buf, sems) = refs[:-5], refs[-5:]
    share = y_out.shape[0]
    y_at = pl.ds(pl.multiple_of(table_ref[2 * slots + 2] * share, share), share)
    y_copy = pltpu.make_async_copy(y_ref.at[y_at], y_out, sems.at[0])
    y_copy.start()
    places, sub, width = other_ref.shape
    part = sub // 4
    v = other_ref[...].reshape(places * sub, width)
    hi = v.astype(jnp.bfloat16)
    mid = (v - hi.astype(jnp.float32)).astype(jnp.bfloat16)
    dims = (((0,), (0,)), ((), ()))
    acc = lax.dot_general(hi, mid, dims, preferred_element_type=jnp.float32)
    acc += lax.dot_general(mid, hi, dims, preferred_element_type=jnp.float32)
    acc += lax.dot_general(hi, hi, dims, preferred_element_type=jnp.float32)
    gram_buf[...] = (gram_ref[...] + acc) * (1.0 / (RB_DEV * BLK))
    gram_copy = pltpu.make_async_copy(gram_buf, gram_out, sems.at[1])
    gram_copy.start()

    own = table_ref[2 * slots + 1] == 0
    acc_ref[...] = jnp.zeros_like(acc_ref)
    for s in range(slots):

        @pl.when(s < table_ref[2 * slots])
        def _():
            row = table_ref[s]
            at = pl.ds(pl.multiple_of(row % 2 * (2 * part), 2 * part), 2 * part)
            parts = []
            for odd in range(2):
                mine, theirs = own_ref[odd * (RB_DEV // 2) + row // 2, at, :], other_ref[odd * (RB_DEV // 2) + row // 2, at, :]
                parts.append(jnp.where(own, mine, theirs).reshape(2, part, width))
                parts.append(jnp.where(own, theirs, mine).reshape(2, part, width))
            y_block = jnp.stack(parts, axis=1).reshape(BLK, width)
            base = pl.multiple_of(table_ref[slots + s] * BLK, BLK)
            acc_ref[pl.ds(base, BLK), :] += tile_dot(tile_ref[s], y_block, 0)

    at = 0
    for ref in out_refs:
        ref[...] = acc_ref[at : at + ref.shape[0], :]
        at += ref.shape[0]
    y_copy.wait()
    gram_copy.wait()


def join_kernel(*refs):
    pieces, (z_ref, sems) = refs[:-2], refs[-2:]
    copies, at = [], 0
    for i, ref in enumerate(pieces):
        copies.append(pltpu.make_async_copy(ref, z_ref.at[at : at + ref.shape[0]], sems.at[i]))
        at += ref.shape[0]
    for copy in copies:
        copy.start()
    for copy in copies:
        copy.wait()


VMEM = pl.BlockSpec(memory_space=pltpu.VMEM)
SMEM = pl.BlockSpec(memory_space=pltpu.SMEM)
ANY = pl.BlockSpec(memory_space=pl.ANY)
PARAMS = pltpu.CompilerParams(vmem_limit_bytes=16 << 20)


def make_local(nx, ny, nc):
    def local(tile_values, tile_rows, tile_cols, live_counts, test_block):
        f32 = jnp.float32
        width = test_block.shape[1]
        panel = RB_DEV * BLK
        share = panel // (nx * ny * nc)
        half = panel // nc
        tiles = tile_values[0, 0]
        core = lax.axis_index("core").astype(jnp.int32)[None]
        place = lax.axis_index("pair").astype(jnp.int32)[None]
        scalars = (tile_rows[0, 0], tile_cols[0, 0], live_counts[0], core)
        swap = [(0, 1), (1, 0)]

        half_shape = pltpu.VMEM((half, width), f32)
        share_of = pl.pallas_call(
            sample_kernel,
            out_shape=half_shape,
            in_specs=[SMEM] * 4 + [VMEM] * 2,
            out_specs=VMEM,
            cost_estimate=pl.CostEstimate(flops=1 << 27, transcendentals=0, bytes_accessed=3 << 20),
            name="sample",
        )
        send = share_of(*scalars[:3], 1 - core, tiles, test_block)
        keep = share_of(*scalars, tiles, test_block)
        part = keep + lax.ppermute(send, "core", swap)
        near, far = nx * 2, ny // 2
        part = part.reshape(near, half // near, width)
        part = lax.all_to_all(part, ("odd", "x"), 0, 0, tiled=True).sum(0)
        chunk = lax.all_gather(part, "pair", axis=0, tiled=False).sum(0)
        own = jnp.broadcast_to(chunk[None], (near, far * share, width))
        own = lax.all_to_all(own, ("odd", "x"), 0, 0, tiled=True)
        other = lax.ppermute(own, "core", swap)

        flat = own.reshape(half, width)
        gram = jnp.dot(flat.T, flat, precision=lax.Precision.HIGH, preferred_element_type=f32)

        table = jnp.concatenate(scalars + (place,))
        rows_out = CB_DEV * BLK
        step = rows_out // PIECES
        sizes = [step] * (PIECES - 1) + [step // 2] * 2
        *pieces, gram, y_out = pl.pallas_call(
            power_kernel,
            out_shape=tuple(jax.ShapeDtypeStruct((n, width), f32) for n in sizes)
            + (
                jax.ShapeDtypeStruct((width, width), f32),
                jax.ShapeDtypeStruct((share, width), f32),
            ),
            in_specs=[SMEM] + [VMEM] * 5,
            out_specs=tuple(VMEM for _ in sizes) + (ANY, ANY),
            scratch_shapes=[
                pltpu.VMEM((rows_out, width), f32),
                pltpu.VMEM((width, width), f32),
                pltpu.SemaphoreType.DMA((2,)),
            ],
            compiler_params=PARAMS,
            name="power",
        )(table, tiles, own, other, gram, chunk)
        pieces = lax.psum(pieces, "z")
        z_power = pl.pallas_call(
            join_kernel,
            out_shape=jax.ShapeDtypeStruct((rows_out, width), f32),
            in_specs=[VMEM] * len(sizes),
            out_specs=ANY,
            scratch_shapes=[pltpu.SemaphoreType.DMA((len(sizes),))],
            compiler_params=PARAMS,
            name="join",
        )(*pieces)
        return (y_out, z_power, gram[None])

    return local


def solution(mesh):
    rows, cols = mesh.shape["rows"], mesh.shape["cols"]
    ny, nc = 8, 2
    nx = cols // (ny * nc)
    grid = Mesh(mesh.devices.reshape(rows, nx, ny // 2, 2, nc), ("z", "x", "pair", "odd", "core"))
    split = ("x", "pair", "odd", "core")
    return jax.shard_map(
        make_local(nx, ny, nc),
        mesh=grid,
        in_specs=(
            P("z", split, None, None, None),
            P("z", split, None),
            P("z", split, None),
            P("z", split),
            P(split, None),
        ),
        out_specs=(P(("z",) + split, None), P(split, None), P("z", None, None)),
        check_vma=False,
    )
```

```python
import jax
import jax.numpy as jnp
from jax import lax
from jax.experimental import pallas as pl
from jax.experimental.pallas import tpu as pltpu
from jax.sharding import Mesh, PartitionSpec as P

RB_DEV = 8
CB_DEV = 4
BLK = 128
PIECES = 64


def tile_dot(tile, v, axis):
    hi = v.astype(jnp.bfloat16)
    mid = (v - hi.astype(jnp.float32)).astype(jnp.bfloat16)
    dims = (((axis,), (0,)), ((), ()))
    return lax.dot_general(
        jnp.concatenate([tile, tile], axis=axis),
        jnp.concatenate([hi, mid], axis=0),
        dims,
        preferred_element_type=jnp.float32,
    )


def sample_kernel(rows_ref, cols_ref, live_ref, core_ref, tile_ref, omega_ref, out_ref):
    lower = core_ref[0] == 0
    width = omega_ref.shape[1]
    sub = out_ref.shape[0] // RB_DEV
    part = sub // 4
    out_ref[...] = jnp.zeros_like(out_ref)
    for s in range(tile_ref.shape[0]):

        @pl.when(s < live_ref[0])
        def _():
            base = pl.multiple_of(cols_ref[s] * BLK, BLK)
            tile = tile_ref[s].reshape(4, 2, part, BLK)
            tile = jnp.where(lower, tile[:, 0], tile[:, 1]).reshape(sub, BLK)
            prod = tile_dot(tile, omega_ref[pl.ds(base, BLK), :], 1).reshape(2, 2, part, width)
            row = rows_ref[s]
            for odd in range(2):
                at = (odd * (RB_DEV // 2) + row // 2) * sub + row % 2 * (2 * part)
                at = pl.ds(pl.multiple_of(at, 2 * part), 2 * part)
                out_ref[at, :] += prod[:, odd].reshape(2 * part, width)


def power_kernel(
    table_ref, tile_ref, own_ref, other_ref, gram_ref, y_ref, *refs
):
    slots = tile_ref.shape[0]
    out_refs, (gram_out, y_out, acc_ref, gram_buf, sems) = refs[:-5], refs[-5:]
    share = y_out.shape[0]
    y_at = pl.ds(pl.multiple_of(table_ref[2 * slots + 2] * share, share), share)
    y_copy = pltpu.make_async_copy(y_ref.at[y_at], y_out, sems.at[0])
    y_copy.start()
    places, sub, width = other_ref.shape
    part = sub // 4
    v = other_ref[...].reshape(places * sub, width)
    hi = v.astype(jnp.bfloat16)
    mid = (v - hi.astype(jnp.float32)).astype(jnp.bfloat16)
    dims = (((0,), (0,)), ((), ()))
    acc = lax.dot_general(
        jnp.concatenate([hi, mid, hi], axis=0),
        jnp.concatenate([mid, hi, hi], axis=0),
        dims,
        preferred_element_type=jnp.float32,
    )
    gram_buf[...] = (gram_ref[...] + acc) * (1.0 / (RB_DEV * BLK))
    gram_copy = pltpu.make_async_copy(gram_buf, gram_out, sems.at[1])
    gram_copy.start()

    own = table_ref[2 * slots + 1] == 0
    acc_ref[...] = jnp.zeros_like(acc_ref)
    for s in range(slots):

        @pl.when(s < table_ref[2 * slots])
        def _():
            row = table_ref[s]
            at = pl.ds(pl.multiple_of(row % 2 * (2 * part), 2 * part), 2 * part)
            parts = []
            for odd in range(2):
                mine, theirs = own_ref[odd * (RB_DEV // 2) + row // 2, at, :], other_ref[odd * (RB_DEV // 2) + row // 2, at, :]
                parts.append(jnp.where(own, mine, theirs).reshape(2, part, width))
                parts.append(jnp.where(own, theirs, mine).reshape(2, part, width))
            y_block = jnp.stack(parts, axis=1).reshape(BLK, width)
            base = pl.multiple_of(table_ref[slots + s] * BLK, BLK)
            acc_ref[pl.ds(base, BLK), :] += tile_dot(tile_ref[s], y_block, 0)

    at = 0
    for ref in out_refs:
        ref[...] = acc_ref[at : at + ref.shape[0], :]
        at += ref.shape[0]
    y_copy.wait()
    gram_copy.wait()


def join_kernel(*refs):
    pieces, (z_ref, sems) = refs[:-2], refs[-2:]
    copies, at = [], 0
    for i, ref in enumerate(pieces):
        copies.append(pltpu.make_async_copy(ref, z_ref.at[at : at + ref.shape[0]], sems.at[i]))
        at += ref.shape[0]
    for copy in copies:
        copy.start()
    for copy in copies:
        copy.wait()


VMEM = pl.BlockSpec(memory_space=pltpu.VMEM)
SMEM = pl.BlockSpec(memory_space=pltpu.SMEM)
ANY = pl.BlockSpec(memory_space=pl.ANY)
PARAMS = pltpu.CompilerParams(vmem_limit_bytes=16 << 20)


def make_local(nx, ny, nc):
    def local(tile_values, tile_rows, tile_cols, live_counts, test_block):
        f32 = jnp.float32
        width = test_block.shape[1]
        panel = RB_DEV * BLK
        share = panel // (nx * ny * nc)
        half = panel // nc
        tiles = tile_values[0, 0]
        core = lax.axis_index("core").astype(jnp.int32)[None]
        place = lax.axis_index("pair").astype(jnp.int32)[None]
        scalars = (tile_rows[0, 0], tile_cols[0, 0], live_counts[0], core)
        swap = [(0, 1), (1, 0)]

        half_shape = pltpu.VMEM((half, width), f32)
        share_of = pl.pallas_call(
            sample_kernel,
            out_shape=half_shape,
            in_specs=[SMEM] * 4 + [VMEM] * 2,
            out_specs=VMEM,
            cost_estimate=pl.CostEstimate(flops=1 << 27, transcendentals=0, bytes_accessed=3 << 20),
            name="sample",
        )
        send = share_of(*scalars[:3], 1 - core, tiles, test_block)
        keep = share_of(*scalars, tiles, test_block)
        part = keep + lax.ppermute(send, "core", swap)
        near, far = nx * 2, ny // 2
        part = part.reshape(near, half // near, width)
        part = lax.all_to_all(part, ("odd", "x"), 0, 0, tiled=True).sum(0)
        chunk = lax.all_gather(part, "pair", axis=0, tiled=False).sum(0)
        own = jnp.broadcast_to(chunk[None], (near, far * share, width))
        own = lax.all_to_all(own, ("odd", "x"), 0, 0, tiled=True)
        other = lax.ppermute(own, "core", swap)

        flat = own.reshape(half, width)
        gram = jnp.dot(flat.T, flat, precision=lax.Precision.HIGH, preferred_element_type=f32)

        table = jnp.concatenate(scalars + (place,))
        rows_out = CB_DEV * BLK
        step = rows_out // PIECES
        sizes = [step] * (PIECES - 1) + [step // 2] * 2
        *pieces, gram, y_out = pl.pallas_call(
            power_kernel,
            out_shape=tuple(jax.ShapeDtypeStruct((n, width), f32) for n in sizes)
            + (
                jax.ShapeDtypeStruct((width, width), f32),
                jax.ShapeDtypeStruct((share, width), f32),
            ),
            in_specs=[SMEM] + [VMEM] * 5,
            out_specs=tuple(VMEM for _ in sizes) + (ANY, ANY),
            scratch_shapes=[
                pltpu.VMEM((rows_out, width), f32),
                pltpu.VMEM((width, width), f32),
                pltpu.SemaphoreType.DMA((2,)),
            ],
            compiler_params=PARAMS,
            name="power",
        )(table, tiles, own, other, gram, chunk)
        pieces = lax.psum(pieces, "z")
        z_power = pl.pallas_call(
            join_kernel,
            out_shape=jax.ShapeDtypeStruct((rows_out, width), f32),
            in_specs=[VMEM] * len(sizes),
            out_specs=ANY,
            scratch_shapes=[pltpu.SemaphoreType.DMA((len(sizes),))],
            compiler_params=PARAMS,
            name="join",
        )(*pieces)
        return (y_out, z_power, gram[None])

    return local


def solution(mesh):
    rows, cols = mesh.shape["rows"], mesh.shape["cols"]
    ny, nc = 8, 2
    nx = cols // (ny * nc)
    grid = Mesh(mesh.devices.reshape(rows, nx, ny // 2, 2, nc), ("z", "x", "pair", "odd", "core"))
    split = ("x", "pair", "odd", "core")
    return jax.shard_map(
        make_local(nx, ny, nc),
        mesh=grid,
        in_specs=(
            P("z", split, None, None, None),
            P("z", split, None),
            P("z", split, None),
            P("z", split),
            P(split, None),
        ),
        out_specs=(P(("z",) + split, None), P(split, None), P("z", None, None)),
        check_vma=False,
    )
```
